512 devices in a mesh: dp: 32 (over x_lo, z), mp: 16 (over y, x_hi, core).
Axes of the slice: x: 4 (x_hi: 2, x_lo: 2; x = x_hi * 2 + x_lo), y: 4, z: 16, core: 2. Of those that a mesh axis runs over, the one named last changes fastest.
Arguments:
- activations: bfloat16 [32, 1024, 512], P('dp', 'mp'), may hold values from -6 to 6
- filters: bfloat16 [27, 1024, 1024], P(None, 'mp', 'dp'), may hold values from -0.0390625 to 0.0390625
- bias: float32 [1024], P('mp'), may hold values from -3 to 3
Outputs:
- features: bfloat16 [32, 1024, 512], P('dp', 'mp')
The draws below stay inside these ranges and needn't reach their ends.
All inputs are finite; a program needn't handle non-finite values.
Results may differ from the reference program's by a relative error of at most 0.001.
Values may be sent and summed in bfloat16 or wider, within the bound.
No kernel may reach another device: no remote copies, remote signals or barrier semaphores. Data moves between devices by JAX's collectives and lax.ppermute only.
A program may use at most 128 MiB of HBM per device.

```python
import jax
import jax.numpy as jnp
from jax import lax

CIN = 1024
COUT = 1024
TAPS = 27
SX = 2
SY = 16
SZ = 16
CELLS = 512
SAMPLES = 32


def levels(stream_key, shape, cuts, smallest, largest):
    factor_of = 1.0
    for dim, shards_of in cuts:
        draws = jax.random.uniform(jax.random.fold_in(jax.random.fold_in(stream_key, 6), dim), (shards_of,), jnp.float32, smallest / len(cuts), largest / len(cuts))
        factor_of = factor_of * jnp.repeat(jnp.exp(draws), shape[dim] // shards_of).reshape((-1,) + (1,) * (len(shape) - 1 - dim))
    return factor_of


def scatter_about(stream_key, extent, deviation, most, split=(), kind=jnp.bfloat16):
    drawn = deviation * jax.random.normal(stream_key, extent, jnp.float32)
    if split:
        drawn = drawn * levels(stream_key, extent, split, -0.22, 0.18)
    return jnp.clip(drawn, -most, most).astype(kind)


def setup_inputs(seed: int = 0) -> dict:
    arg_keys = jax.random.split(jax.random.key(seed), 4)
    activations = scatter_about(arg_keys[0], (SAMPLES, CIN, CELLS), 1.0, 6.0, ((0, 32), (1, 16)))
    filters = scatter_about(arg_keys[1], (TAPS, COUT, CIN), (TAPS * CIN) ** -0.5, 0.0390625, ((1, 16), (2, 32)))
    bias = scatter_about(arg_keys[2], (COUT,), 0.5, 3.0, ((0, 16),), jnp.float32)
    return dict(activations=activations, filters=filters, bias=bias)


def shifted(values, off_a, off_b, off_c):
    cells = SX * SY * SZ
    margin = SY * SZ + SZ + 1
    extended = jnp.pad(values, ((0, 0), (margin, margin)))
    offset = off_a * SY * SZ + off_b * SZ + off_c
    moved = extended[:, margin + offset:margin + offset + cells]
    place = jnp.arange(cells, dtype=jnp.int32)
    first = place // (SY * SZ) + off_a
    second = (place // SZ) % SY + off_b
    third = place % SZ + off_c
    inside = (first >= 0) & (first < SX) & (second >= 0) & (second < SY) & (third >= 0) & (third < SZ)
    return jnp.where(inside[None, :], moved, jnp.zeros_like(moved))


def one_sample(inputs, filters, bias):
    summed = jnp.zeros((COUT, SX * SY * SZ), jnp.float32)
    for off_a in (-1, 0, 1):
        for off_b in (-1, 0, 1):
            for off_c in (-1, 0, 1):
                tap = 9 * (off_a + 1) + 3 * (off_b + 1) + (off_c + 1)
                moved = shifted(inputs, off_a, off_b, off_c)
                summed = summed + jnp.dot(filters[tap], moved, preferred_element_type=jnp.float32)
    value = summed + bias[:, None]
    return jnp.where(value > 0, value, 0.3 * value).astype(jnp.bfloat16)


def reference(activations, filters, bias):
    return lax.map(lambda inputs: one_sample(inputs, filters, bias), activations)
```

```python
import functools

import jax
import jax.numpy as jnp
from jax import lax
from jax.experimental import pallas as pl
from jax.experimental.pallas import tpu as pltpu
from jax.sharding import Mesh, PartitionSpec as P

PLANE = 256
ROW = 16
IN_PLANE = 9
CHUNK = 32
CHUNKS = 16


def pack_kernel(taps_ref, out_ref):
    out_ref[:, :CHUNK, :] = jnp.concatenate([taps_ref[9:18], taps_ref[0:9]], axis=2)
    out_ref[:, CHUNK:, :] = jnp.concatenate([taps_ref[18:27, :16], taps_ref[18:27, 16:]], axis=2)


def pack(filters):
    by_tap = jnp.transpose(filters, (0, 2, 1))
    return pl.pallas_call(
        pack_kernel,
        out_shape=jax.ShapeDtypeStruct((IN_PLANE, 48, 128), jnp.bfloat16),
        name="pack",
    )(by_tap)


def conv_kernel(where_ref, same_ref, before_ref, after_ref, mine_ref, other_ref, part_ref, weights, columns):
    parity = where_ref[0]
    core = where_ref[1]

    def place(block, row):
        for tap in range(IN_PLANE):
            pair = block[tap, :CHUNK, :]
            last = block[tap, CHUNK:, :]
            lanes = slice(tap * 128, tap * 128 + 128)
            weights[row : row + CHUNK, lanes] = pair
            third = jnp.concatenate([last[:, :64], last[:, 64:]], axis=0)
            weights[512 + row : 512 + row + CHUNK, lanes] = jnp.concatenate([third, pair[:, :64]], axis=1)

    for m in range(8):
        place(same_ref[m], m * CHUNK)
        place(before_ref[m] if m < 4 else after_ref[m - 4], 256 + m * CHUNK)

    place_in_row = lax.broadcasted_iota(jnp.int32, (PLANE, 128), 0) % ROW
    zeros = jnp.zeros((ROW, 128), jnp.float32)
    for s in range(2):
        for m in range(8):
            pair = s * 4 + m // 2
            for turn in range(2):
                rows = pl.ds(pl.multiple_of(CHUNK * (parity if turn == 0 else 1 - parity), CHUNK), CHUNK)
                at = turn * 256 + m * CHUNK
                here = core == m % 2
                cells = jnp.where(here, mine_ref[pair, rows, :], other_ref[pair, rows, :])
                columns[at : at + CHUNK, :] = cells[:, :PLANE]
                columns[512 + at : 512 + at + CHUNK, :] = cells[:, PLANE:]
        taps = lax.dot_general(
            columns[...], weights[...], (((0,), (0,)), ((), ())), preferred_element_type=jnp.float32
        )

        def tap_of(b, c):
            lane = (3 * (b + 1) + (c + 1)) * 128
            return taps[:, lane : lane + 128]

        def rows_summed(c):
            up = jnp.concatenate([tap_of(1, c)[ROW:], zeros], axis=0)
            down = jnp.concatenate([zeros, tap_of(-1, c)[:-ROW]], axis=0)
            return tap_of(0, c) + up + down

        right = jnp.where(place_in_row < ROW - 1, pltpu.roll(rows_summed(1), PLANE - 1, 0), 0.0)
        left = jnp.where(place_in_row > 0, pltpu.roll(rows_summed(-1), 1, 0), 0.0)
        part_ref[s] = rows_summed(0) + right + left


def conv(where, same, before, after, mine, other):
    vmem = pl.BlockSpec(memory_space=pltpu.VMEM)
    return pl.pallas_call(
        conv_kernel,
        in_specs=[pl.BlockSpec(memory_space=pltpu.SMEM)] + [vmem] * 5,
        out_specs=vmem,
        out_shape=jax.ShapeDtypeStruct((2, PLANE, 128), jnp.float32),
        scratch_shapes=[
            pltpu.VMEM((1024, IN_PLANE * 128), jnp.bfloat16),
            pltpu.VMEM((1024, PLANE), jnp.bfloat16),
        ],
        compiler_params=pltpu.CompilerParams(vmem_limit_bytes=48 * 2**20),
        cost_estimate=pl.CostEstimate(flops=1_300_000_000, bytes_accessed=4_000_000, transcendentals=0),
        name="conv",
    )(where, same, before, after, mine, other)


def finish_kernel(mine_ref, partner_ref, bias_ref, out_ref):
    bias = bias_ref[...]
    value = mine_ref[...] + partner_ref[...] + jnp.concatenate([bias, bias], axis=1)
    value = jnp.where(value > 0, value, 0.3 * value)
    turned = value.T.astype(jnp.bfloat16)
    out_ref[0, :, :PLANE] = turned[:64]
    out_ref[0, :, PLANE:] = turned[64:]


def finish(mine, partner, bias):
    return pl.pallas_call(
        finish_kernel,
        out_shape=jax.ShapeDtypeStruct((1, 64, 2 * PLANE), jnp.bfloat16),
        name="finish",
    )(mine, partner, bias.reshape(1, 64))


def swap_places():
    moves = []
    for xl in range(2):
        for y in range(4):
            half = y // 2
            moves.append((xl * 4 + y, half * 4 + (y if half == xl else (y + 2) % 4)))
    return moves


def ring(step):
    return [(i, (i + step) % CHUNKS) for i in range(CHUNKS)]


def per_device(activations, filters, bias):
    z = lax.axis_index("z")
    core = lax.axis_index("core")
    xl = lax.axis_index("xl")

    block = lax.ppermute(activations, ("xl", "y"), swap_places())
    packed = pack(filters)
    same = lax.all_gather(
        packed, "z", axis_index_groups=[list(range(0, CHUNKS, 2)), list(range(1, CHUNKS, 2))]
    )
    before = lax.ppermute(same[:4], "z", ring(1))
    after = lax.ppermute(same[4:], "z", ring(-1))
    mine = lax.all_to_all(jnp.broadcast_to(block, (8, 64, 512)), ("y", "xh"), 0, 0, tiled=True)
    other = lax.ppermute(mine, "core", [(0, 1), (1, 0)])
    parts = conv(jnp.stack([z % 2, core]).astype(jnp.int32), same, before, after, mine, other)
    own = lax.dynamic_index_in_dim(parts, xl, 0, keepdims=False)
    lent = lax.dynamic_index_in_dim(parts, 1 - xl, 0, keepdims=False)
    partner = lax.ppermute(lent, "xl", [(0, 1), (1, 0)])
    return finish(own, partner, bias)


def solution(mesh):
    fine = Mesh(mesh.devices.reshape(2, 16, 4, 2, 2), ("xl", "z", "y", "xh", "core"))
    dp, mp = ("xl", "z"), ("y", "xh", "core")
    return jax.shard_map(
        per_device,
        mesh=fine,
        in_specs=(P(dp, mp, None), P(None, mp, dp), P(mp)),
        out_specs=P(dp, mp, None),
        check_vma=False,
    )
```

```python
import jax
import jax.numpy as jnp
from jax import lax
from jax.experimental import pallas as pl
from jax.experimental.pallas import tpu as pltpu
from jax.sharding import Mesh, PartitionSpec as P

PLANE = 256
ROW = 16
IN_PLANE = 9
CHUNK = 32
CHUNKS = 8


def pack_kernel(taps_ref, out_ref):
    out_ref[:, :CHUNK, :] = jnp.concatenate([taps_ref[9:18], taps_ref[0:9]], axis=2)
    out_ref[:, CHUNK:, :] = jnp.concatenate([taps_ref[18:27, :16], taps_ref[18:27, 16:]], axis=2)


def pack(filters):
    by_tap = jnp.transpose(filters, (0, 2, 1))
    return pl.pallas_call(
        pack_kernel,
        out_shape=jax.ShapeDtypeStruct((IN_PLANE, 48, 128), jnp.bfloat16),
        name="pack",
    )(by_tap)


def conv_kernel(where_ref, blocks_ref, cells_ref, part_ref, weights, columns):
    zp = where_ref[0]

    for m in range(CHUNKS):
        row = m * CHUNK
        for tap in range(IN_PLANE):
            pair = blocks_ref[m, tap, :CHUNK, :]
            last = blocks_ref[m, tap, CHUNK:, :]
            lanes = slice(tap * 128, tap * 128 + 128)
            weights[row : row + CHUNK, lanes] = pair
            third = jnp.concatenate([last[:, :64], last[:, 64:]], axis=0)
            weights[256 + row : 256 + row + CHUNK, lanes] = jnp.concatenate([third, pair[:, :64]], axis=1)

    place_in_row = lax.broadcasted_iota(jnp.int32, (PLANE, 128), 0) % ROW
    zeros = jnp.zeros((ROW, 128), jnp.float32)
    for slot in range(2):
        for xl in range(2):
            for m in range(CHUNKS):
                cells = cells_ref[xl * CHUNKS + m, slot]
                columns[m * CHUNK : (m + 1) * CHUNK, :] = cells[:, :PLANE]
                columns[256 + m * CHUNK : 256 + (m + 1) * CHUNK, :] = cells[:, PLANE:]
            taps = lax.dot_general(
                columns[...], weights[...], (((0,), (0,)), ((), ())), preferred_element_type=jnp.float32
            )

            def tap_of(b, c, taps=taps):
                lane = (3 * (b + 1) + (c + 1)) * 128
                return taps[:, lane : lane + 128]

            def rows_summed(c, tap_of=tap_of):
                up = jnp.concatenate([tap_of(1, c)[ROW:], zeros], axis=0)
                down = jnp.concatenate([zeros, tap_of(-1, c)[:-ROW]], axis=0)
                return tap_of(0, c) + up + down

            right = jnp.where(place_in_row < ROW - 1, pltpu.roll(rows_summed(1), PLANE - 1, 0), 0.0)
            left = jnp.where(place_in_row > 0, pltpu.roll(rows_summed(-1), 1, 0), 0.0)
            part_ref[2 * (zp if slot == 0 else 1 - zp) + xl] = rows_summed(0) + right + left


def conv(where, blocks, cells):
    vmem = pl.BlockSpec(memory_space=pltpu.VMEM)
    return pl.pallas_call(
        conv_kernel,
        in_specs=[pl.BlockSpec(memory_space=pltpu.SMEM), vmem, vmem],
        out_specs=vmem,
        out_shape=jax.ShapeDtypeStruct((4, PLANE, 128), jnp.float32),
        scratch_shapes=[
            pltpu.VMEM((512, IN_PLANE * 128), jnp.bfloat16),
            pltpu.VMEM((512, PLANE), jnp.bfloat16),
        ],
        compiler_params=pltpu.CompilerParams(vmem_limit_bytes=32 * 2**20),
        cost_estimate=pl.CostEstimate(flops=1_300_000_000, bytes_accessed=3_000_000, transcendentals=0),
        name="conv",
    )(where, blocks, cells)


def finish_kernel(parts_ref, bias_ref, out_ref):
    bias = bias_ref[...]
    value = (parts_ref[0] + parts_ref[1]) + (parts_ref[2] + parts_ref[3])
    value = value + jnp.concatenate([bias, bias], axis=1)
    value = jnp.where(value > 0, value, 0.3 * value)
    turned = value.T.astype(jnp.bfloat16)
    out_ref[0, :, :PLANE] = turned[:64]
    out_ref[0, :, PLANE:] = turned[64:]


def finish(parts, bias):
    return pl.pallas_call(
        finish_kernel,
        out_shape=jax.ShapeDtypeStruct((1, 64, 2 * PLANE), jnp.bfloat16),
        name="finish",
    )(parts, bias.reshape(1, 64))


def moves(other_z):
    pairs = []
    for xl in range(2):
        for zp in range(2):
            for y in range(4):
                half = y // 2
                there = y if half == xl else (y + 2) % 4
                to = 1 - zp if other_z else zp
                pairs.append(((xl * 2 + zp) * 4 + y, (half * 2 + to) * 4 + there))
    return pairs


def per_device(activations, filters, bias):
    zp = lax.axis_index("zp")
    rows = activations.reshape(2, CHUNK, 512)
    kept = lax.dynamic_index_in_dim(rows, zp, 0, keepdims=False)
    lent = lax.dynamic_index_in_dim(rows, 1 - zp, 0, keepdims=False)
    kept = lax.ppermute(kept, ("xl", "zp", "y"), moves(False))
    lent = lax.ppermute(lent, ("xl", "zp", "y"), moves(True))
    packed = pack(filters)
    pieces = jnp.broadcast_to(jnp.stack([kept, lent]), (16, 2, CHUNK, 512))
    cells = lax.all_to_all(pieces, ("y", "xh", "core"), 0, 0, tiled=True)
    blocks = lax.all_gather(packed, "zh")
    parts = conv(zp.astype(jnp.int32).reshape(1), blocks, cells)
    parts = lax.all_to_all(parts, ("zp", "xl"), 0, 0, tiled=True)
    return finish(parts, bias)


def solution(mesh):
    fine = Mesh(mesh.devices.reshape(2, 8, 2, 4, 2, 2), ("xl", "zh", "zp", "y", "xh", "core"))
    dp, mp = ("xl", "zh", "zp"), ("y", "xh", "core")
    return jax.shard_map(
        per_device,
        mesh=fine,
        in_specs=(P(dp, mp, None), P(None, mp, dp), P(mp)),
        out_specs=P(dp, mp, None),
        check_vma=False,
    )
```

```python
import jax
import jax.numpy as jnp
from jax import lax
from jax.experimental import pallas as pl
from jax.experimental.pallas import tpu as pltpu
from jax.sharding import Mesh, PartitionSpec as P

PLANE = 256
ROW = 16
IN_PLANE = 9
CHUNK = 32
CHUNKS = 8


def pack_kernel(taps_ref, out_ref):
    out_ref[:, :CHUNK, :] = jnp.concatenate([taps_ref[9:18], taps_ref[0:9]], axis=2)
    out_ref[:, CHUNK:, :] = jnp.concatenate([taps_ref[18:27, :16], taps_ref[18:27, 16:]], axis=2)


def pack(filters):
    by_tap = jnp.transpose(filters, (0, 2, 1))
    return pl.pallas_call(
        pack_kernel,
        out_shape=jax.ShapeDtypeStruct((IN_PLANE, 48, 128), jnp.bfloat16),
        name="pack",
    )(by_tap)


def conv_kernel(where_ref, blocks_ref, cells_ref, part_ref, weights, columns):
    zp = where_ref[0]
    half = where_ref[1]

    for m in range(CHUNKS):
        row = m * CHUNK
        for tap in range(IN_PLANE):
            pair = blocks_ref[m, tap, :CHUNK, :]
            last = blocks_ref[m, tap, CHUNK:, :]
            lanes = slice(tap * 128, tap * 128 + 128)
            weights[row : row + CHUNK, lanes] = pair
            third = jnp.concatenate([last[:, :64], last[:, 64:]], axis=0)
            weights[256 + row : 256 + row + CHUNK, lanes] = jnp.concatenate([third, pair[:, :64]], axis=1)

    place_in_row = lax.broadcasted_iota(jnp.int32, (PLANE, 128), 0) % ROW
    zeros = jnp.zeros((ROW, 128), jnp.float32)
    for slot in range(2):
        for xl in range(2):
            for m in range(CHUNKS):
                cells = cells_ref[xl * 16 + 8 * half + m, slot]
                columns[m * CHUNK : (m + 1) * CHUNK, :] = cells[:, :PLANE]
                columns[256 + m * CHUNK : 256 + (m + 1) * CHUNK, :] = cells[:, PLANE:]
            taps = lax.dot_general(
                columns[...], weights[...], (((0,), (0,)), ((), ())), preferred_element_type=jnp.float32
            )

            def tap_of(b, c, taps=taps):
                lane = (3 * (b + 1) + (c + 1)) * 128
                return taps[:, lane : lane + 128]

            def rows_summed(c, tap_of=tap_of):
                up = jnp.concatenate([tap_of(1, c)[ROW:], zeros], axis=0)
                down = jnp.concatenate([zeros, tap_of(-1, c)[:-ROW]], axis=0)
                return tap_of(0, c) + up + down

            right = jnp.where(place_in_row < ROW - 1, pltpu.roll(rows_summed(1), PLANE - 1, 0), 0.0)
            left = jnp.where(place_in_row > 0, pltpu.roll(rows_summed(-1), 1, 0), 0.0)
            part_ref[2 * (zp if slot == 0 else 1 - zp) + xl] = rows_summed(0) + right + left


def conv(where, blocks, cells):
    vmem = pl.BlockSpec(memory_space=pltpu.VMEM)
    return pl.pallas_call(
        conv_kernel,
        in_specs=[pl.BlockSpec(memory_space=pltpu.SMEM), vmem, vmem],
        out_specs=vmem,
        out_shape=jax.ShapeDtypeStruct((4, PLANE, 128), jnp.float32),
        scratch_shapes=[
            pltpu.VMEM((512, IN_PLANE * 128), jnp.bfloat16),
            pltpu.VMEM((512, PLANE), jnp.bfloat16),
        ],
        compiler_params=pltpu.CompilerParams(vmem_limit_bytes=32 * 2**20),
        cost_estimate=pl.CostEstimate(flops=1_300_000_000, bytes_accessed=3_000_000, transcendentals=0),
        name="conv",
    )(where, blocks, cells)


def finish_kernel(parts_ref, bias_ref, out_ref):
    bias = bias_ref[...]
    value = (parts_ref[0] + parts_ref[1]) + (parts_ref[2] + parts_ref[3])
    value = value + jnp.concatenate([bias, bias], axis=1)
    value = jnp.where(value > 0, value, 0.3 * value)
    turned = value.T.astype(jnp.bfloat16)
    out_ref[0, :, :PLANE] = turned[:64]
    out_ref[0, :, PLANE:] = turned[64:]


def finish(parts, bias):
    return pl.pallas_call(
        finish_kernel,
        out_shape=jax.ShapeDtypeStruct((1, 64, 2 * PLANE), jnp.bfloat16),
        name="finish",
    )(parts, bias.reshape(1, 64))


def per_device(activations, filters, bias):
    xl, zp = lax.axis_index("xl"), lax.axis_index("zp")
    rows = activations.reshape(2, CHUNK, 512)
    kept = lax.dynamic_index_in_dim(rows, zp, 0, keepdims=False)
    lent = lax.dynamic_index_in_dim(rows, 1 - zp, 0, keepdims=False)
    lent = lax.ppermute(lent, "zp", [(0, 1), (1, 0)])
    packed = pack(filters)
    lent, packed = lax.optimization_barrier((lent, packed))
    pieces = jnp.broadcast_to(jnp.stack([kept, lent]), (32, 2, CHUNK, 512))
    cells = lax.all_to_all(pieces, ("xl", "y", "xh", "core"), 0, 0, tiled=True)
    blocks = lax.all_gather(packed, "zh")
    parts = conv(jnp.stack([zp, xl]).astype(jnp.int32), blocks, cells)
    parts = lax.all_to_all(parts, ("zp", "xl"), 0, 0, tiled=True)
    return finish(parts, bias)


def solution(mesh):
    fine = Mesh(mesh.devices.reshape(2, 8, 2, 4, 2, 2), ("xl", "zh", "zp", "y", "xh", "core"))
    dp, mp = ("xl", "zh", "zp"), ("y", "xh", "core")
    return jax.shard_map(
        per_device,
        mesh=fine,
        in_specs=(P(dp, mp, None), P(None, mp, dp), P(mp)),
        out_specs=P(dp, mp, None),
        check_vma=False,
    )
```

```python
import jax
import jax.numpy as jnp
from jax import lax
from jax.experimental import pallas as pl
from jax.experimental.pallas import tpu as pltpu
from jax.sharding import Mesh, PartitionSpec as P

PLANE = 256
ROW = 16
IN_PLANE = 9
CHUNK = 32
CHUNKS = 8
PLACES = 32


def own_rows():
    return pl.ds(pl.multiple_of(lax.axis_index("zp") * CHUNK, CHUNK), CHUNK)


def pack_kernel(taps_ref, own_ref, out_ref, kept_ref):
    out_ref[:, :CHUNK, :] = jnp.concatenate([taps_ref[9:18], taps_ref[0:9]], axis=2)
    out_ref[:, CHUNK:, :] = jnp.concatenate([taps_ref[18:27, :16], taps_ref[18:27, 16:]], axis=2)
    kept_ref[...] = own_ref[0, own_rows(), :]


def pack(filters, activations):
    by_tap = jnp.transpose(filters, (0, 2, 1))
    return pl.pallas_call(
        pack_kernel,
        out_shape=(
            jax.ShapeDtypeStruct((IN_PLANE, 48, 128), jnp.bfloat16),
            jax.ShapeDtypeStruct((CHUNK, 512), jnp.bfloat16),
        ),
        compiler_params=pltpu.CompilerParams(vmem_limit_bytes=4 * 2**20),
        name="pack",
    )(by_tap, activations)


def spread_kernel(kept_ref, partner_ref, pieces_ref):
    kept = kept_ref[...]
    lent = partner_ref[0, own_rows(), :]
    for i in range(PLACES):
        pieces_ref[i, 0] = kept
        pieces_ref[i, 1] = lent


def spread(kept, partner):
    return pl.pallas_call(
        spread_kernel,
        out_shape=jax.ShapeDtypeStruct((PLACES, 2, CHUNK, 512), jnp.bfloat16),
        compiler_params=pltpu.CompilerParams(vmem_limit_bytes=4 * 2**20),
        name="spread",
    )(kept, partner)


def conv_kernel(blocks_ref, cells_ref, part_ref, weights, columns):
    zp, half = lax.axis_index("zp"), lax.axis_index("xl")

    for m in range(CHUNKS):
        row = m * CHUNK
        for tap in range(IN_PLANE):
            pair = blocks_ref[m, tap, :CHUNK, :]
            last = blocks_ref[m, tap, CHUNK:, :]
            lanes = slice(tap * 128, tap * 128 + 128)
            weights[row : row + CHUNK, lanes] = pair
            third = jnp.concatenate([last[:, :64], last[:, 64:]], axis=0)
            weights[256 + row : 256 + row + CHUNK, lanes] = jnp.concatenate([third, pair[:, :64]], axis=1)

    place_in_row = lax.broadcasted_iota(jnp.int32, (PLANE, 128), 0) % ROW
    zeros = jnp.zeros((ROW, 128), jnp.float32)
    for slot in range(2):
        for xl in range(2):
            for m in range(CHUNKS):
                cells = cells_ref[xl * 16 + 8 * half + m, slot]
                columns[m * CHUNK : (m + 1) * CHUNK, :] = cells[:, :PLANE]
                columns[256 + m * CHUNK : 256 + (m + 1) * CHUNK, :] = cells[:, PLANE:]
            taps = lax.dot_general(
                columns[...], weights[...], (((0,), (0,)), ((), ())), preferred_element_type=jnp.float32
            )

            def tap_of(b, c, taps=taps):
                lane = (3 * (b + 1) + (c + 1)) * 128
                return taps[:, lane : lane + 128]

            def rows_summed(c, tap_of=tap_of):
                up = jnp.concatenate([tap_of(1, c)[ROW:], zeros], axis=0)
                down = jnp.concatenate([zeros, tap_of(-1, c)[:-ROW]], axis=0)
                return tap_of(0, c) + up + down

            right = jnp.where(place_in_row < ROW - 1, pltpu.roll(rows_summed(1), PLANE - 1, 0), 0.0)
            left = jnp.where(place_in_row > 0, pltpu.roll(rows_summed(-1), 1, 0), 0.0)
            part_ref[2 * (zp if slot == 0 else 1 - zp) + xl] = rows_summed(0) + right + left


def conv(blocks, cells):
    vmem = pl.BlockSpec(memory_space=pltpu.VMEM)
    return pl.pallas_call(
        conv_kernel,
        in_specs=[vmem, vmem],
        out_specs=vmem,
        out_shape=jax.ShapeDtypeStruct((4, PLANE, 128), jnp.float32),
        scratch_shapes=[
            pltpu.VMEM((512, IN_PLANE * 128), jnp.bfloat16),
            pltpu.VMEM((512, PLANE), jnp.bfloat16),
        ],
        compiler_params=pltpu.CompilerParams(vmem_limit_bytes=32 * 2**20),
        cost_estimate=pl.CostEstimate(flops=1_300_000_000, bytes_accessed=3_000_000, transcendentals=0),
        name="conv",
    )(blocks, cells)


def finish_kernel(parts_ref, bias_ref, out_ref):
    bias = bias_ref[...]
    value = (parts_ref[0] + parts_ref[1]) + (parts_ref[2] + parts_ref[3])
    value = value + jnp.concatenate([bias, bias], axis=1)
    value = jnp.where(value > 0, value, 0.3 * value)
    turned = value.T.astype(jnp.bfloat16)
    out_ref[0, :, :PLANE] = turned[:64]
    out_ref[0, :, PLANE:] = turned[64:]


def finish(parts, bias):
    return pl.pallas_call(
        finish_kernel,
        out_shape=jax.ShapeDtypeStruct((1, 64, 2 * PLANE), jnp.bfloat16),
        compiler_params=pltpu.CompilerParams(vmem_limit_bytes=4 * 2**20),
        name="finish",
    )(parts, bias.reshape(1, 64))


def per_device(activations, filters, bias):
    partner = lax.ppermute(activations, "zp", [(0, 1), (1, 0)])
    packed, kept = pack(filters, activations)
    partner, packed = lax.optimization_barrier((partner, packed))
    cells = lax.all_to_all(spread(kept, partner), ("xl", "y", "xh", "core"), 0, 0, tiled=True)
    blocks = lax.all_gather(packed, "zh")
    parts = lax.all_to_all(conv(blocks, cells), ("zp", "xl"), 0, 0, tiled=True)
    return finish(parts, bias)


def solution(mesh):
    fine = Mesh(mesh.devices.reshape(2, 8, 2, 4, 2, 2), ("xl", "zh", "zp", "y", "xh", "core"))
    dp, mp = ("xl", "zh", "zp"), ("y", "xh", "core")
    return jax.shard_map(
        per_device,
        mesh=fine,
        in_specs=(P(dp, mp, None), P(None, mp, dp), P(mp)),
        out_specs=P(dp, mp, None),
        check_vma=False,
    )
```

```python
import jax
import jax.numpy as jnp
from jax import lax
from jax.experimental import pallas as pl
from jax.experimental.pallas import tpu as pltpu
from jax.sharding import Mesh, PartitionSpec as P

PLANE = 256
ROW = 16
IN_PLANE = 9
CHUNK = 32
CHUNKS = 8
PLACES = 32


def pack_kernel(taps_ref, out_ref):
    out_ref[:, :CHUNK, :] = jnp.concatenate([taps_ref[9:18], taps_ref[0:9]], axis=2)
    out_ref[:, CHUNK:, :] = jnp.concatenate([taps_ref[18:27, :16], taps_ref[18:27, 16:]], axis=2)


def pack(filters):
    by_tap = jnp.transpose(filters, (0, 2, 1))
    return pl.pallas_call(
        pack_kernel,
        out_shape=jax.ShapeDtypeStruct((IN_PLANE, 48, 128), jnp.bfloat16),
        compiler_params=pltpu.CompilerParams(vmem_limit_bytes=4 * 2**20),
        name="pack",
    )(by_tap)


def spread_kernel(rows_ref, pieces_ref):
    rows = rows_ref[...]
    for i in range(PLACES):
        pieces_ref[i] = rows


def spread(rows):
    return pl.pallas_call(
        spread_kernel,
        out_shape=jax.ShapeDtypeStruct((PLACES, 2, CHUNK, 512), jnp.bfloat16),
        compiler_params=pltpu.CompilerParams(vmem_limit_bytes=4 * 2**20),
        name="spread",
    )(rows)


def conv_kernel(blocks_ref, cells_ref, part_ref, weights, columns):
    half = lax.axis_index("xl")

    for m in range(CHUNKS):
        row = m * CHUNK
        for tap in range(IN_PLANE):
            pair = blocks_ref[m, tap, :CHUNK, :]
            last = blocks_ref[m, tap, CHUNK:, :]
            lanes = slice(tap * 128, tap * 128 + 128)
            weights[row : row + CHUNK, lanes] = pair
            third = jnp.concatenate([last[:, :64], last[:, 64:]], axis=0)
            weights[256 + row : 256 + row + CHUNK, lanes] = jnp.concatenate([third, pair[:, :64]], axis=1)

    place_in_row = lax.broadcasted_iota(jnp.int32, (PLANE, 128), 0) % ROW
    zeros = jnp.zeros((ROW, 128), jnp.float32)
    for slot in range(2):
        for xl in range(2):
            for m in range(CHUNKS):
                cells = cells_ref[xl * 16 + 8 * half + m, slot]
                columns[m * CHUNK : (m + 1) * CHUNK, :] = cells[:, :PLANE]
                columns[256 + m * CHUNK : 256 + (m + 1) * CHUNK, :] = cells[:, PLANE:]
            taps = lax.dot_general(
                columns[...], weights[...], (((0,), (0,)), ((), ())), preferred_element_type=jnp.float32
            )

            def tap_of(b, c, taps=taps):
                lane = (3 * (b + 1) + (c + 1)) * 128
                return taps[:, lane : lane + 128]

            def rows_summed(c, tap_of=tap_of):
                up = jnp.concatenate([tap_of(1, c)[ROW:], zeros], axis=0)
                down = jnp.concatenate([zeros, tap_of(-1, c)[:-ROW]], axis=0)
                return tap_of(0, c) + up + down

            right = jnp.where(place_in_row < ROW - 1, pltpu.roll(rows_summed(1), PLANE - 1, 0), 0.0)
            left = jnp.where(place_in_row > 0, pltpu.roll(rows_summed(-1), 1, 0), 0.0)
            part_ref[2 * slot + xl] = rows_summed(0) + right + left


def conv(blocks, cells):
    vmem = pl.BlockSpec(memory_space=pltpu.VMEM)
    return pl.pallas_call(
        conv_kernel,
        in_specs=[vmem, vmem],
        out_specs=vmem,
        out_shape=jax.ShapeDtypeStruct((4, PLANE, 128), jnp.float32),
        scratch_shapes=[
            pltpu.VMEM((512, IN_PLANE * 128), jnp.bfloat16),
            pltpu.VMEM((512, PLANE), jnp.bfloat16),
        ],
        compiler_params=pltpu.CompilerParams(vmem_limit_bytes=32 * 2**20),
        cost_estimate=pl.CostEstimate(flops=1_300_000_000, bytes_accessed=3_000_000, transcendentals=0),
        name="conv",
    )(blocks, cells)


def finish_kernel(parts_ref, bias_ref, out_ref):
    bias = bias_ref[...]
    value = (parts_ref[0] + parts_ref[1]) + (parts_ref[2] + parts_ref[3])
    value = value + jnp.concatenate([bias, bias], axis=1)
    value = jnp.where(value > 0, value, 0.3 * value)
    turned = value.T.astype(jnp.bfloat16)
    out_ref[0, :, :PLANE] = turned[:64]
    out_ref[0, :, PLANE:] = turned[64:]


def finish(parts, bias):
    return pl.pallas_call(
        finish_kernel,
        out_shape=jax.ShapeDtypeStruct((1, 64, 2 * PLANE), jnp.bfloat16),
        compiler_params=pltpu.CompilerParams(vmem_limit_bytes=4 * 2**20),
        name="finish",
    )(parts, bias.reshape(1, 64))


def per_device(activations, filters, bias):
    packed = pack(filters)
    rows = lax.all_to_all(activations.reshape(2, CHUNK, 512), "zp", 0, 0, tiled=True)
    rows, packed = lax.optimization_barrier((rows, packed))
    cells = lax.all_to_all(spread(rows), ("xl", "y", "xh", "core"), 0, 0, tiled=True)
    blocks = lax.all_gather(packed, "zh")
    parts = lax.all_to_all(conv(blocks, cells), ("zp", "xl"), 0, 0, tiled=True)
    return finish(parts, bias)


def solution(mesh):
    fine = Mesh(mesh.devices.reshape(2, 8, 2, 4, 2, 2), ("xl", "zh", "zp", "y", "xh", "core"))
    dp, mp = ("xl", "zh", "zp"), ("y", "xh", "core")
    return jax.shard_map(
        per_device,
        mesh=fine,
        in_specs=(P(dp, mp, None), P(None, mp, dp), P(mp)),
        out_specs=P(dp, mp, None),
        check_vma=False,
    )
```

```python
import jax
import jax.numpy as jnp
from jax import lax
from jax.experimental import pallas as pl
from jax.experimental.pallas import tpu as pltpu
from jax.sharding import Mesh, PartitionSpec as P

PLANE = 256
ROW = 16
IN_PLANE = 9
CHUNK = 32
CHUNKS = 8
PLACES = 32


def pack_kernel(taps_ref, out_ref):
    out_ref[:, :CHUNK, :] = jnp.concatenate([taps_ref[9:18], taps_ref[0:9]], axis=2)
    out_ref[:, CHUNK:, :] = jnp.concatenate([taps_ref[18:27, :16], taps_ref[18:27, 16:]], axis=2)


def pack(filters):
    by_tap = jnp.transpose(filters, (0, 2, 1))
    return pl.pallas_call(
        pack_kernel,
        out_shape=jax.ShapeDtypeStruct((IN_PLANE, 48, 128), jnp.bfloat16),
        compiler_params=pltpu.CompilerParams(vmem_limit_bytes=4 * 2**20),
        name="pack",
    )(by_tap)


def spread_kernel(rows_ref, pieces_ref):
    rows = rows_ref[...]
    for i in range(PLACES):
        pieces_ref[i] = rows


def spread(rows):
    return pl.pallas_call(
        spread_kernel,
        out_shape=jax.ShapeDtypeStruct((PLACES, 2, CHUNK, 512), jnp.bfloat16),
        compiler_params=pltpu.CompilerParams(vmem_limit_bytes=4 * 2**20),
        name="spread",
    )(rows)


def conv_kernel(blocks_ref, cells_ref, part_ref, weights, columns):
    half = lax.axis_index("xl")

    for m in range(CHUNKS):
        row = m * CHUNK
        for tap in range(IN_PLANE):
            pair = blocks_ref[m, tap, :CHUNK, :]
            last = blocks_ref[m, tap, CHUNK:, :]
            lanes = slice(tap * 128, tap * 128 + 128)
            weights[row : row + CHUNK, lanes] = pair
            third = jnp.concatenate([last[:, :64], last[:, 64:]], axis=0)
            weights[256 + row : 256 + row + CHUNK, lanes] = jnp.concatenate([third, pair[:, :64]], axis=1)

    place_in_row = lax.broadcasted_iota(jnp.int32, (PLANE, 128), 0) % ROW
    zeros = jnp.zeros((ROW, 128), jnp.float32)
    for slot in range(2):
        for xl in range(2):
            at = slice(xl * PLANE, (xl + 1) * PLANE)
            for m in range(CHUNKS):
                cells = cells_ref[xl * 16 + 8 * half + m, slot]
                columns[m * CHUNK : (m + 1) * CHUNK, at] = cells[:, :PLANE]
                columns[256 + m * CHUNK : 256 + (m + 1) * CHUNK, at] = cells[:, PLANE:]
        taps = lax.dot_general(
            columns[...], weights[...], (((0,), (0,)), ((), ())), preferred_element_type=jnp.float32
        )
        for xl in range(2):

            def tap_of(b, c, rows=taps[xl * PLANE : (xl + 1) * PLANE]):
                lane = (3 * (b + 1) + (c + 1)) * 128
                return rows[:, lane : lane + 128]

            def rows_summed(c, tap_of=tap_of):
                up = jnp.concatenate([tap_of(1, c)[ROW:], zeros], axis=0)
                down = jnp.concatenate([zeros, tap_of(-1, c)[:-ROW]], axis=0)
                return tap_of(0, c) + up + down

            right = jnp.where(place_in_row < ROW - 1, pltpu.roll(rows_summed(1), PLANE - 1, 0), 0.0)
            left = jnp.where(place_in_row > 0, pltpu.roll(rows_summed(-1), 1, 0), 0.0)
            part_ref[2 * slot + xl] = rows_summed(0) + right + left


def conv(blocks, cells):
    vmem = pl.BlockSpec(memory_space=pltpu.VMEM)
    return pl.pallas_call(
        conv_kernel,
        in_specs=[vmem, vmem],
        out_specs=vmem,
        out_shape=jax.ShapeDtypeStruct((4, PLANE, 128), jnp.float32),
        scratch_shapes=[
            pltpu.VMEM((512, IN_PLANE * 128), jnp.bfloat16),
            pltpu.VMEM((512, 2 * PLANE), jnp.bfloat16),
        ],
        compiler_params=pltpu.CompilerParams(vmem_limit_bytes=32 * 2**20),
        cost_estimate=pl.CostEstimate(flops=1_300_000_000, bytes_accessed=3_000_000, transcendentals=0),
        name="conv",
    )(blocks, cells)


def finish_kernel(parts_ref, bias_ref, out_ref):
    bias = bias_ref[...]
    value = (parts_ref[0] + parts_ref[1]) + (parts_ref[2] + parts_ref[3])
    value = value + jnp.concatenate([bias, bias], axis=1)
    value = jnp.where(value > 0, value, 0.3 * value)
    turned = value.T.astype(jnp.bfloat16)
    out_ref[0, :, :PLANE] = turned[:64]
    out_ref[0, :, PLANE:] = turned[64:]


def finish(parts, bias):
    return pl.pallas_call(
        finish_kernel,
        out_shape=jax.ShapeDtypeStruct((1, 64, 2 * PLANE), jnp.bfloat16),
        compiler_params=pltpu.CompilerParams(vmem_limit_bytes=4 * 2**20),
        name="finish",
    )(parts, bias.reshape(1, 64))


def per_device(activations, filters, bias):
    packed = pack(filters)
    rows = lax.all_to_all(activations.reshape(2, CHUNK, 512), "zp", 0, 0, tiled=True)
    rows, packed = lax.optimization_barrier((rows, packed))
    cells = lax.all_to_all(spread(rows), ("xl", "y", "xh", "core"), 0, 0, tiled=True)
    blocks = lax.all_gather(packed.reshape(432, 128), "zh", axis=0, tiled=True).reshape(8, 9, 48, 128)
    parts = lax.all_to_all(conv(blocks, cells), ("zp", "xl"), 0, 0, tiled=True)
    return finish(parts, bias)


def solution(mesh):
    fine = Mesh(mesh.devices.reshape(2, 8, 2, 4, 2, 2), ("xl", "zh", "zp", "y", "xh", "core"))
    dp, mp = ("xl", "zh", "zp"), ("y", "xh", "core")
    return jax.shard_map(
        per_device,
        mesh=fine,
        in_specs=(P(dp, mp, None), P(None, mp, dp), P(mp)),
        out_specs=P(dp, mp, None),
        check_vma=False,
    )
```

```python
import jax
import jax.numpy as jnp
from jax import lax
from jax.experimental import pallas as pl
from jax.experimental.pallas import tpu as pltpu
from jax.sharding import Mesh, PartitionSpec as P

PLANE = 256
ROW = 16
IN_PLANE = 9
CHUNK = 32
CHUNKS = 8
PLACES = 32


def pack_kernel(taps_ref, out_ref):
    out_ref[:, :CHUNK, :] = jnp.concatenate([taps_ref[9:18], taps_ref[0:9]], axis=2)
    out_ref[:, CHUNK:, :] = jnp.concatenate([taps_ref[18:27, :16], taps_ref[18:27, 16:]], axis=2)


def pack(filters):
    by_tap = jnp.transpose(filters, (0, 2, 1))
    return pl.pallas_call(
        pack_kernel,
        out_shape=jax.ShapeDtypeStruct((IN_PLANE, 48, 128), jnp.bfloat16),
        compiler_params=pltpu.CompilerParams(vmem_limit_bytes=4 * 2**20),
        name="pack",
    )(by_tap)


def conv_kernel(blocks_ref, cells_ref, part_ref, weights, columns):
    half = lax.axis_index("xl")

    for m in range(CHUNKS):
        row = m * CHUNK
        for tap in range(IN_PLANE):
            pair = blocks_ref[m, tap, :CHUNK, :]
            last = blocks_ref[m, tap, CHUNK:, :]
            lanes = slice(tap * 128, tap * 128 + 128)
            weights[row : row + CHUNK, lanes] = pair
            third = jnp.concatenate([last[:, :64], last[:, 64:]], axis=0)
            weights[256 + row : 256 + row + CHUNK, lanes] = jnp.concatenate([third, pair[:, :64]], axis=1)

    place_in_row = lax.broadcasted_iota(jnp.int32, (PLANE, 128), 0) % ROW
    zeros = jnp.zeros((ROW, 128), jnp.float32)
    for slot in range(2):
        for xl in range(2):
            at = slice(xl * PLANE, (xl + 1) * PLANE)
            for m in range(CHUNKS):
                cells = cells_ref[xl * 16 + 8 * half + m, slot]
                columns[m * CHUNK : (m + 1) * CHUNK, at] = cells[:, :PLANE]
                columns[256 + m * CHUNK : 256 + (m + 1) * CHUNK, at] = cells[:, PLANE:]
        taps = lax.dot_general(
            columns[...], weights[...], (((0,), (0,)), ((), ())), preferred_element_type=jnp.float32
        )
        for xl in range(2):

            def tap_of(b, c, rows=taps[xl * PLANE : (xl + 1) * PLANE]):
                lane = (3 * (b + 1) + (c + 1)) * 128
                return rows[:, lane : lane + 128]

            def rows_summed(c, tap_of=tap_of):
                up = jnp.concatenate([tap_of(1, c)[ROW:], zeros], axis=0)
                down = jnp.concatenate([zeros, tap_of(-1, c)[:-ROW]], axis=0)
                return tap_of(0, c) + up + down

            right = jnp.where(place_in_row < ROW - 1, pltpu.roll(rows_summed(1), PLANE - 1, 0), 0.0)
            left = jnp.where(place_in_row > 0, pltpu.roll(rows_summed(-1), 1, 0), 0.0)
            part_ref[2 * slot + xl] = rows_summed(0) + right + left


def conv(blocks, cells):
    vmem = pl.BlockSpec(memory_space=pltpu.VMEM)
    return pl.pallas_call(
        conv_kernel,
        in_specs=[vmem, vmem],
        out_specs=vmem,
        out_shape=jax.ShapeDtypeStruct((4, PLANE, 128), jnp.float32),
        scratch_shapes=[
            pltpu.VMEM((512, IN_PLANE * 128), jnp.bfloat16),
            pltpu.VMEM((512, 2 * PLANE), jnp.bfloat16),
        ],
        compiler_params=pltpu.CompilerParams(vmem_limit_bytes=32 * 2**20),
        cost_estimate=pl.CostEstimate(flops=1_300_000_000, bytes_accessed=3_000_000, transcendentals=0),
        name="conv",
    )(blocks, cells)


def finish_kernel(parts_ref, bias_ref, out_ref):
    bias = bias_ref[...]
    value = (parts_ref[0] + parts_ref[1]) + (parts_ref[2] + parts_ref[3])
    value = value + jnp.concatenate([bias, bias], axis=1)
    value = jnp.where(value > 0, value, 0.3 * value)
    turned = value.T.astype(jnp.bfloat16)
    out_ref[0, :, :PLANE] = turned[:64]
    out_ref[0, :, PLANE:] = turned[64:]


def finish(parts, bias):
    return pl.pallas_call(
        finish_kernel,
        out_shape=jax.ShapeDtypeStruct((1, 64, 2 * PLANE), jnp.bfloat16),
        compiler_params=pltpu.CompilerParams(vmem_limit_bytes=4 * 2**20),
        name="finish",
    )(parts, bias.reshape(1, 64))


def per_device(activations, filters, bias):
    packed = pack(filters)
    rows = lax.all_to_all(activations.reshape(2, CHUNK, 512), "zp", 0, 0, tiled=True)
    rows, packed = lax.optimization_barrier((rows, packed))
    cells = lax.all_to_all(jnp.broadcast_to(rows, (PLACES, 2, CHUNK, 512)), ("xl", "y", "xh", "core"), 0, 0, tiled=True)
    blocks = lax.all_gather(packed.reshape(432, 128), "zh", axis=0, tiled=True).reshape(8, 9, 48, 128)
    parts = lax.all_to_all(conv(blocks, cells), ("zp", "xl"), 0, 0, tiled=True)
    return finish(parts, bias)


def solution(mesh):
    fine = Mesh(mesh.devices.reshape(2, 8, 2, 4, 2, 2), ("xl", "zh", "zp", "y", "xh", "core"))
    dp, mp = ("xl", "zh", "zp"), ("y", "xh", "core")
    return jax.shard_map(
        per_device,
        mesh=fine,
        in_specs=(P(dp, mp, None), P(None, mp, dp), P(mp)),
        out_specs=P(dp, mp, None),
        check_vma=False,
    )
```
